32 devices in a mesh: groups: 2 (over x), tm: 8 (over z, y), space: 2 (over core).
Axes of the slice: x: 2, y: 2, z: 4, core: 2. Of those that a mesh axis runs over, the one named last changes fastest.
Arguments:
- latents: bfloat16 [32, 12, 80, 2240], P(('groups', 'tm'), 'space'), parts along dimension 0, may hold values from -8 to 8
- proj_weight: bfloat16 [2240, 3360], P('tm'), may hold values from -0.125 to 0.125
Outputs:
- attended: bfloat16 [32, 12, 80, 1120], P(('groups', 'tm'), 'space'), parts along dimension 0
The draws below stay inside these ranges and needn't reach their ends.
There are 2 independent parts, one for each index of `groups`. The reference program is written for one: setup_inputs(seed, part) draws one part's arguments, and reference() takes and returns one part's arrays. A program takes and returns all parts, laid end to end along the dimension named above; an argument that names none is the same for every part. Nothing has to cross between parts.
All inputs are finite; a program needn't handle non-finite values.
Results may differ from the reference program's by a relative error of at most 0.0034.
Values may be sent and summed in bfloat16 or wider, within the bound.
A program may use at most 128 MiB of HBM per device.

```python
import jax
import jax.numpy as jnp
from jax import lax

D = 2240
HEADS = 10
HEAD = 112
WIDTH = 80
F_DEV = 2
FRAMES = 16
ROWS = 12


def draw_latents(key, part):
    key_scene = jax.random.fold_in(key, 11)
    key_region = jax.random.fold_in(key, 12)
    key_jitter = jax.random.fold_in(key, 13)
    scenes = jax.random.normal(key_scene, (FRAMES, 1, 1, D), jnp.float32)
    jitter = jax.random.normal(key_jitter, (FRAMES, ROWS, WIDTH, D), jnp.float32)
    region = 0.5 * jax.random.normal(key_region, (1, ROWS, 1, D), jnp.float32)
    return jnp.clip(scenes + region + jitter, -8.0, 8.0).astype(jnp.bfloat16)


def block_levels(own_key, dims, split, least, high):
    loudness = 1.0
    for position, blocks in split:
        steps = jax.random.uniform(jax.random.fold_in(jax.random.fold_in(own_key, 6), position), (blocks,), jnp.float32, least / len(split), high / len(split))
        loudness = loudness * jnp.repeat(jnp.exp(steps), dims[position] // blocks).reshape((-1,) + (1,) * (len(dims) - 1 - position))
    return loudness


def bell_draw(own_key, dims, width, reach, pieces=(), held_as=jnp.bfloat16):
    result = jax.random.normal(own_key, dims, jnp.float32) * width
    if len(pieces) > 0:
        result = block_levels(own_key, dims, pieces, -0.22, 0.18) * result
    return jnp.clip(result, min=-reach, max=reach).astype(held_as)


def setup_inputs(seed: int = 0, part: int = 0) -> dict:
    key_of = jax.random.split(jax.random.key(seed), 3)
    own_keys = jax.random.split(jax.random.fold_in(key_of[2], part), 3)
    return {
        "latents": draw_latents(jax.random.fold_in(jax.random.fold_in(key_of[2], part), 71), part),
        "proj_weight": bell_draw(key_of[1], (D, 3 * HEADS * HEAD), D ** -0.5, 0.125, ((0, 8),)),
    }


def block_states(projected_block):
    key_feats = jax.nn.relu(projected_block[:, 1]).astype(jnp.float32)
    values = projected_block[:, 2].astype(jnp.float32)
    states = jnp.einsum("nhe,nhf->hef", key_feats, values)
    key_sums = jnp.sum(key_feats, axis=0)
    return states, key_sums


def attend_block(operands):
    projected_block, states, key_sums = operands
    queries = jax.nn.relu(projected_block[:, 0]).astype(jnp.float32)
    rounded = lax.optimization_barrier(states.astype(jnp.bfloat16)).astype(jnp.float32)
    numerator = jnp.einsum("nhe,hef->nhf", queries, rounded)
    denominator = jnp.einsum("nhe,he->nh", queries, key_sums, precision=lax.Precision.HIGHEST)
    return (numerator / (denominator[:, :, None] + 1.0)).astype(jnp.bfloat16)


def reference(latents, proj_weight):
    frame_count, row_count, column_count, channels = latents.shape
    per_block = F_DEV * row_count * column_count
    block_count = frame_count // F_DEV
    tokens = latents.reshape(block_count, per_block, channels)

    def project(frame_block):
        return jnp.dot(frame_block, proj_weight, preferred_element_type=jnp.float32).astype(jnp.bfloat16)

    projected = lax.map(project, tokens).reshape(block_count, per_block, 3, HEADS, HEAD)
    states, key_sums = lax.map(block_states, projected)
    total_states = jnp.cumsum(states, axis=0)
    total_sums = jnp.cumsum(key_sums, axis=0)
    attended = lax.map(attend_block, (projected, total_states, total_sums))
    return attended.reshape(frame_count, row_count, column_count, HEADS * HEAD)
```

```python
import functools

import jax
import jax.numpy as jnp
from jax import lax
from jax.experimental import pallas as pl
from jax.experimental.pallas import tpu as pltpu
from jax.sharding import PartitionSpec as P

HEADS = 10
HEAD = 112
LANES = 128
CLASSES = 3
MESH = pl.DeviceIdType.MESH


def round_plan(tiles):
    plan, first = [], 0
    while tiles - first >= 2 * CLASSES:
        plan.append((first, CLASSES))
        first += 2 * CLASSES
    while tiles - first > 0:
        plan.append((first, 2))
        first += 4
    return plan


def gather_kernel(plan, deep, wide, x_hbm, w_ref, p_ref, buf, x_vm, w_vm,
                  x_sem, own_sem, load_sem, zs, zr, ys, yr, xs, xr, cs, cr):
    group, t, core = lax.axis_index("groups"), lax.axis_index("tm"), lax.axis_index("space")
    z, y = t // wide, t % wide
    own_class = group % 2
    depth = w_ref.shape[0]
    x_peer = {"groups": group + 1 - 2 * own_class}
    y_peer = {"tm": z * wide + 1 - y}
    core_peer = {"space": 1 - core}

    def z_at(dz):
        return lax.rem(z + deep - dz, deep)

    barrier = pltpu.get_barrier_semaphore()
    peers = [x_peer, y_peer, core_peer]
    peers += [{"tm": lax.rem(z + dz, deep) * wide + y} for dz in range(1, deep)]
    for peer in peers:
        pl.semaphore_signal(barrier, inc=1, device_id=peer, device_id_type=MESH)

    x_copy = pltpu.make_async_copy(x_hbm, x_vm, x_sem)
    x_copy.start()

    def cols(r, kind, parity):
        return pl.ds(pl.multiple_of((plan[r][0] + 2 * kind + parity) * LANES, LANES), LANES)

    def rows(shard):
        return pl.ds(pl.multiple_of(shard * depth, 8), depth)

    def kind_of(s):
        return own_class if s == 0 else 2

    def fetched(r):
        return range(plan[r][1] - 1)

    own = {}
    for r, (first, kinds) in enumerate(plan):
        for kind in range(kinds):
            c = cols(r, kind, core)
            own[r, kind] = pltpu.make_async_copy(
                w_ref.at[:, c], buf.at[rows(t), c], own_sem.at[r, kind])
            own[r, kind].start()

    pl.semaphore_wait(barrier, len(peers))

    def remote(src, dst, send, recv, peer):
        return pltpu.make_async_remote_copy(
            src_ref=src, dst_ref=dst, send_sem=send, recv_sem=recv,
            device_id=peer, device_id_type=MESH)

    def z_copy(r, s, dz):
        c = cols(r, kind_of(s), core)
        return remote(w_ref.at[:, c], buf.at[rows(t), c], zs.at[r, s, dz], zr.at[r, s, dz],
                      {"tm": lax.rem(z + dz, deep) * wide + y})

    def y_copy(r, s, dz):
        c = cols(r, kind_of(s), core)
        at = buf.at[rows(z_at(dz) * wide + y), c]
        return remote(w_ref.at[:, c] if dz == 0 else at, at, ys.at[r, s, dz], yr.at[r, s, dz], y_peer)

    def x_copy_of(r, dz, side):
        c = cols(r, own_class, core)
        at = buf.at[rows(z_at(dz) * wide + (y if side == 0 else 1 - y)), c]
        return remote(at, at, xs.at[r, side, dz], xr.at[r, side, dz], x_peer)

    def core_copy(r, s):
        kind = own_class if s == 0 else (2 if s == 1 else 1 - own_class)
        at = buf.at[:, cols(r, kind, core)]
        return remote(at, at, cs.at[r, s], cr.at[r, s], core_peer)

    sent = []

    def start(copy):
        copy.start()
        sent.append(copy)

    def send_own(r):
        for s in fetched(r):
            for dz in range(1, deep):
                start(z_copy(r, s, dz))
        for s in fetched(r):
            start(y_copy(r, s, 0))

    def width(r):
        return 2 * plan[r][1] * LANES

    def load(r):
        return pltpu.make_async_copy(
            buf.at[:, pl.ds(plan[r][0] * LANES, width(r))],
            w_vm.at[r % 2, :, pl.ds(0, width(r))], load_sem.at[r % 2])

    step = 2 * LANES
    block = 240

    def multiply(r, piece):
        first = plan[r][0] * LANES + piece * step

        def body(i, carry):
            at = pl.ds(pl.multiple_of(i * block, block), block)
            p_ref[at, first:first + step] = jnp.dot(
                x_vm[at, :], w_vm[r % 2, :, piece * step:(piece + 1) * step],
                preferred_element_type=jnp.float32).astype(p_ref.dtype)
            return carry

        lax.fori_loop(0, x_vm.shape[0] // block, body, 0)

    rounds = len(plan)
    send_own(0)
    x_copy.wait()
    pending = []
    for r in range(rounds + 1):
        if r + 1 < rounds:
            send_own(r + 1)
        if r < rounds:
            for dz in range(1, deep):
                if pending:
                    multiply(*pending.pop(0))
                for s in fetched(r):
                    z_copy(r, s, dz).wait_recv()
                    start(y_copy(r, s, dz))
                    if s == 0:
                        start(x_copy_of(r, dz, 0))
            for dz in range(deep):
                for s in fetched(r):
                    y_copy(r, s, dz).wait_recv()
                    if s == 0:
                        start(x_copy_of(r, dz, 1))
            for kind in range(plan[r][1]):
                own[r, kind].wait()
            for s in fetched(r):
                start(core_copy(r, s))
        for item in pending:
            multiply(*item)
        pending = []
        if r >= 1:
            b = r - 1
            for dz in range(1, deep):
                x_copy_of(b, dz, 0).wait_recv()
            for dz in range(deep):
                x_copy_of(b, dz, 1).wait_recv()
            start(core_copy(b, 2))
            for s in list(fetched(b)) + [2]:
                core_copy(b, s).wait_recv()
            load(b).start()
            load(b).wait()
            pending = [(b, piece) for piece in range(plan[b][1])]
    for item in pending:
        multiply(*item)
    for copy in sent:
        copy.wait_send()


def gather_multiply(x, w, deep, wide):
    tokens, channels = x.shape
    depth, columns = w.shape
    plan = round_plan(columns // LANES)
    rounds = len(plan)
    dma = pltpu.SemaphoreType.DMA
    projected, _ = pl.pallas_call(
        functools.partial(gather_kernel, plan, deep, wide),
        out_shape=(jax.ShapeDtypeStruct((tokens, columns), jnp.bfloat16),
                   jax.ShapeDtypeStruct((channels, columns), jnp.bfloat16)),
        in_specs=[pl.BlockSpec(memory_space=pl.ANY), pl.BlockSpec(memory_space=pltpu.VMEM)],
        out_specs=(pl.BlockSpec(memory_space=pltpu.VMEM), pl.BlockSpec(memory_space=pl.ANY)),
        scratch_shapes=[
            pltpu.VMEM((tokens, channels), jnp.bfloat16),
            pltpu.VMEM((2, channels, 2 * CLASSES * LANES), jnp.bfloat16),
            dma, dma((rounds, CLASSES)), dma((2,)),
            dma((rounds, 2, deep)), dma((rounds, 2, deep)),
            dma((rounds, 2, deep)), dma((rounds, 2, deep)),
            dma((rounds, 2, deep)), dma((rounds, 2, deep)),
            dma((rounds, 3)), dma((rounds, 3)),
        ],
        compiler_params=pltpu.CompilerParams(
            collective_id=0, has_side_effects=True, vmem_limit_bytes=56 * 2 ** 20),
        name="gather_multiply",
    )(x, w)
    return projected


def own_share(states, key_sums):
    both = jnp.concatenate([states, key_sums[:, :, None]], axis=2)
    both = lax.psum(both, "space")
    pieces = lax.all_gather(both, "tm")
    place = lax.broadcasted_iota(jnp.int32, (pieces.shape[0], 1, 1, 1), 0)
    total = jnp.sum(jnp.where(place <= lax.axis_index("tm"), pieces, 0.0), axis=0)
    return total[:, :, :HEAD], total[:, :, HEAD]


def on_device(deep, wide, latents, proj_weight):
    frame_count, band_rows, column_count, channels = latents.shape
    flat = latents.reshape(-1, channels)
    depth, columns = proj_weight.shape
    part = HEADS * HEAD
    queries, keys, values = (proj_weight[:, i * part:(i + 1) * part] for i in range(3))
    if wide:
        room = -(-part // LANES) * LANES
        total = 2 * CLASSES * LANES * ((3 * room) // (2 * CLASSES * LANES))
        total += -(-(3 * room - total) // (4 * LANES)) * 4 * LANES
        gap = ((0, 0), (0, room - part))
        packed = jnp.concatenate(
            [jnp.pad(keys, gap), jnp.pad(values, gap), jnp.pad(queries, ((0, 0), (0, total - 2 * room - part)))], axis=1)
        projected = gather_multiply(flat, packed, deep, wide)
        keys, values, queries = (projected[:, i * room:i * room + part] for i in range(3))
    else:
        full = lax.all_gather(proj_weight, "tm", axis=0, tiled=True)
        projected = jnp.dot(flat, full, preferred_element_type=jnp.float32).astype(jnp.bfloat16)
        queries, keys, values = (projected[:, i * part:(i + 1) * part] for i in range(3))
    queries, keys, values = (a.reshape(-1, HEADS, HEAD) for a in (queries, keys, values))
    queries, keys = jax.nn.relu(queries), jax.nn.relu(keys)
    states = jnp.einsum("nhe,nhf->hef", keys, values, preferred_element_type=jnp.float32)
    key_sums = jnp.sum(keys, axis=0, dtype=jnp.float32)
    states, key_sums = own_share(states, key_sums)
    numerator = jnp.einsum(
        "nhe,hef->nhf", queries, states.astype(jnp.bfloat16), preferred_element_type=jnp.float32)
    denominator = jnp.einsum(
        "nhe,he->nh", queries.astype(jnp.float32), key_sums, precision=lax.Precision.HIGHEST)
    attended = (numerator / (denominator[:, :, None] + 1.0)).astype(jnp.bfloat16)
    return attended.reshape(frame_count, band_rows, column_count, part)


def solution(mesh):
    groups, blocks, bands = (mesh.shape[a] for a in ("groups", "tm", "space"))
    wide = 2

    def body(latents, proj_weight):
        fits = (groups == 2 and bands == 2 and blocks % wide == 0 and proj_weight.shape[0] % 8 == 0)
        return on_device(blocks // wide, wide if fits else 0, latents, proj_weight)

    return jax.shard_map(
        body,
        mesh=mesh,
        in_specs=(P(("groups", "tm"), "space", None, None), P("tm", None)),
        out_specs=P(("groups", "tm"), "space", None, None),
        check_vma=False,
    )
```

```python
import functools

import jax
import jax.numpy as jnp
from jax import lax
from jax.experimental import pallas as pl
from jax.experimental.pallas import tpu as pltpu
from jax.sharding import PartitionSpec as P

HEADS = 10
HEAD = 112
LANES = 128
CLASSES = 3
MESH = pl.DeviceIdType.MESH


def round_plan(tiles):
    plan, first = [], 0
    while tiles - first >= 2 * CLASSES:
        plan.append((first, CLASSES))
        first += 2 * CLASSES
    while tiles - first > 0:
        plan.append((first, 2))
        first += 4
    return plan


def gather_kernel(plan, deep, wide, room, x_hbm, w_ref, o_ref, buf, x_vm, w_vm, p_ref,
                  local, from_core, block_sum, from_y, pair_sum, from_z, to_y, totals, rounded,
                  x_sem, own_sem, load_sem, zs, zr, ys, yr, xs, xr, cs, cr, ss, sr):
    group, t, core = lax.axis_index("groups"), lax.axis_index("tm"), lax.axis_index("space")
    z, y = t // wide, t % wide
    own_class = group % 2
    depth = w_ref.shape[0]
    x_peer = {"groups": group + 1 - 2 * own_class}
    y_peer = {"tm": z * wide + 1 - y}
    core_peer = {"space": 1 - core}

    def z_at(dz):
        return lax.rem(z + deep - dz, deep)

    barrier = pltpu.get_barrier_semaphore()
    peers = [x_peer, y_peer, core_peer]
    peers += [{"tm": lax.rem(z + dz, deep) * wide + y} for dz in range(1, deep)]
    for peer in peers:
        pl.semaphore_signal(barrier, inc=1, device_id=peer, device_id_type=MESH)

    x_copy = pltpu.make_async_copy(x_hbm, x_vm, x_sem)
    x_copy.start()

    def cols(r, kind, parity):
        return pl.ds(pl.multiple_of((plan[r][0] + 2 * kind + parity) * LANES, LANES), LANES)

    def rows(shard):
        return pl.ds(pl.multiple_of(shard * depth, 8), depth)

    def kind_of(s):
        return own_class if s == 0 else 2

    def fetched(r):
        return range(plan[r][1] - 1)

    own = {}
    for r, (first, kinds) in enumerate(plan):
        for kind in range(kinds):
            c = cols(r, kind, core)
            own[r, kind] = pltpu.make_async_copy(
                w_ref.at[:, c], buf.at[rows(t), c], own_sem.at[r, kind])
            own[r, kind].start()

    pl.semaphore_wait(barrier, len(peers))

    def remote(src, dst, send, recv, peer):
        return pltpu.make_async_remote_copy(
            src_ref=src, dst_ref=dst, send_sem=send, recv_sem=recv,
            device_id=peer, device_id_type=MESH)

    def z_copy(r, s, dz):
        c = cols(r, kind_of(s), core)
        return remote(w_ref.at[:, c], buf.at[rows(t), c], zs.at[r, s, dz], zr.at[r, s, dz],
                      {"tm": lax.rem(z + dz, deep) * wide + y})

    def y_copy(r, s, dz):
        c = cols(r, kind_of(s), core)
        at = buf.at[rows(z_at(dz) * wide + y), c]
        return remote(w_ref.at[:, c] if dz == 0 else at, at, ys.at[r, s, dz], yr.at[r, s, dz], y_peer)

    def x_copy_of(r, dz, side):
        c = cols(r, own_class, core)
        at = buf.at[rows(z_at(dz) * wide + (y if side == 0 else 1 - y)), c]
        return remote(at, at, xs.at[r, side, dz], xr.at[r, side, dz], x_peer)

    def core_copy(r, s):
        kind = own_class if s == 0 else (2 if s == 1 else 1 - own_class)
        at = buf.at[:, cols(r, kind, core)]
        return remote(at, at, cs.at[r, s], cr.at[r, s], core_peer)

    sent = []

    def start(copy):
        copy.start()
        sent.append(copy)

    def send_own(r):
        for s in fetched(r):
            for dz in range(1, deep):
                start(z_copy(r, s, dz))
        for s in fetched(r):
            start(y_copy(r, s, 0))

    def width(r):
        return 2 * plan[r][1] * LANES

    def load(r):
        return pltpu.make_async_copy(
            buf.at[:, pl.ds(plan[r][0] * LANES, width(r))],
            w_vm.at[r % 2, :, pl.ds(0, width(r))], load_sem.at[r % 2])

    step = 2 * LANES
    block = 240

    def multiply(r, piece):
        first = plan[r][0] * LANES + piece * step

        def body(i, carry):
            at = pl.ds(pl.multiple_of(i * block, block), block)
            p_ref[at, first:first + step] = jnp.dot(
                x_vm[at, :], w_vm[r % 2, :, piece * step:(piece + 1) * step],
                preferred_element_type=jnp.float32).astype(p_ref.dtype)
            return carry

        lax.fori_loop(0, x_vm.shape[0] // block, body, 0)

    tokens = x_vm.shape[0]
    half = HEADS // 2
    rows_half = HEAD // 2
    my_heads, other_heads = pl.ds(core * half, half), pl.ds((1 - core) * half, half)
    my_rows = pl.ds(pl.multiple_of(y * rows_half, 8), rows_half)
    other_rows = pl.ds(pl.multiple_of((1 - y) * rows_half, 8), rows_half)

    def block_states():
        lane = lax.broadcasted_iota(jnp.int32, (block, LANES), 1)
        for h in range(HEADS):
            def body(i, total):
                at = pl.ds(pl.multiple_of(i * block, block), block)
                keys = jnp.maximum(p_ref[at, h * HEAD:h * HEAD + LANES], 0)
                values = p_ref[at, room + h * HEAD:room + h * HEAD + LANES]
                values = jnp.where(lane < HEAD, values, jnp.ones_like(values))
                return total + lax.dot_general(
                    keys, values, (((0,), (0,)), ((), ())), preferred_element_type=jnp.float32)

            local[h] = lax.fori_loop(0, tokens // block, body, jnp.zeros((LANES, LANES), jnp.float32))[:HEAD]

    def block_states_and_send():
        block_states()
        start(core_sum_copy())

    def core_sum_copy():
        return remote(local.at[other_heads], from_core, ss.at[0], sr.at[0], core_peer)

    def y_sum_copy():
        return remote(block_sum.at[:, other_rows], from_y, ss.at[1], sr.at[1], y_peer)

    def z_sum_copy(dz):
        return remote(pair_sum, from_z.at[dz], ss.at[3 + dz], sr.at[3 + dz],
                      {"tm": lax.rem(z + dz, deep) * wide + y})

    def y_total_copy():
        return remote(to_y, totals.at[my_heads, my_rows], ss.at[2], sr.at[2], y_peer)

    def core_total_copy():
        return remote(totals.at[my_heads], totals.at[my_heads], ss.at[3], sr.at[3], core_peer)

    def exchange_core():
        core_sum_copy().wait_recv()
        block_sum[...] = local[my_heads] + from_core[...]
        start(y_sum_copy())

    def exchange_y():
        y_sum_copy().wait_recv()
        pair_sum[...] = block_sum[:, my_rows] + from_y[...]
        for dz in range(1, deep):
            @pl.when(z + dz < deep)
            def _():
                z_sum_copy(dz).start()

    def exchange_z():
        earlier_me = block_sum[:, my_rows] + jnp.where(y == 0, 0.0, from_y[...])
        earlier_peer = from_y[...] + jnp.where(y == 0, block_sum[:, my_rows], 0.0)
        totals[my_heads, my_rows] = earlier_me
        to_y[...] = earlier_peer
        for dz in range(1, deep):
            @pl.when(z >= dz)
            def _():
                z_sum_copy(dz).wait_recv()
                totals[my_heads, my_rows] += from_z[dz]
                to_y[...] += from_z[dz]
        start(y_total_copy())

    def exchange_back():
        y_total_copy().wait_recv()
        start(core_total_copy())

    def attend():
        core_total_copy().wait_recv()
        lane = lax.broadcasted_iota(jnp.int32, (HEAD, LANES), 1)
        for h in range(HEADS):
            total = totals[h]
            sums = jnp.broadcast_to(total[:, HEAD:HEAD + 1], (HEAD, LANES))
            high = sums.astype(jnp.bfloat16).astype(jnp.float32)
            middle = (sums - high).astype(jnp.bfloat16).astype(jnp.float32)
            low = sums - high - middle
            tail = jnp.where(lane == HEAD, high, jnp.where(lane == HEAD + 1, middle, jnp.where(lane == HEAD + 2, low, 0.0)))
            rounded[h, :HEAD] = jnp.where(lane < HEAD, total, tail).astype(jnp.bfloat16)
            rounded[h, HEAD:] = jnp.zeros((LANES - HEAD, LANES), jnp.bfloat16)

        def body(i, carry):
            at = pl.ds(pl.multiple_of(i * block, block), block)
            for h in range(HEADS):
                first = 2 * room + h * HEAD
                queries = jnp.maximum(p_ref[at, first:first + LANES], 0)
                out = jnp.dot(queries, rounded[h], preferred_element_type=jnp.float32)
                below = out[:, HEAD:HEAD + 1] + out[:, HEAD + 1:HEAD + 2] + out[:, HEAD + 2:HEAD + 3] + 1.0
                o_ref[at, h * HEAD:(h + 1) * HEAD] = (out[:, :HEAD] / below).astype(o_ref.dtype)
            return carry

        lax.fori_loop(0, tokens // block, body, 0)

    rounds = len(plan)
    last_kv = [2 * room <= plan[r][0] * LANES + width(r) for r in range(rounds)].index(True)
    stages = [block_states_and_send, exchange_core, exchange_y, exchange_z, exchange_back]
    done = []

    def advance():
        if len(stages) > len(done):
            stages[len(done)]()
            done.append(1)

    send_own(0)
    x_copy.wait()
    pending = []
    for r in range(rounds + 1):
        if r + 1 < rounds:
            send_own(r + 1)
        if r < rounds:
            for dz in range(1, deep):
                if pending:
                    multiply(*pending.pop(0))
                for s in fetched(r):
                    z_copy(r, s, dz).wait_recv()
                    start(y_copy(r, s, dz))
                    if s == 0:
                        start(x_copy_of(r, dz, 0))
            for dz in range(deep):
                for s in fetched(r):
                    y_copy(r, s, dz).wait_recv()
                    if s == 0:
                        start(x_copy_of(r, dz, 1))
            for kind in range(plan[r][1]):
                own[r, kind].wait()
            for s in fetched(r):
                start(core_copy(r, s))
        for item in pending:
            multiply(*item)
        pending = []
        if r - 2 >= last_kv:
            advance()
        if r >= 1:
            b = r - 1
            for dz in range(1, deep):
                x_copy_of(b, dz, 0).wait_recv()
            for dz in range(deep):
                x_copy_of(b, dz, 1).wait_recv()
            start(core_copy(b, 2))
            for s in list(fetched(b)) + [2]:
                core_copy(b, s).wait_recv()
            load(b).start()
            if r - 2 >= last_kv:
                advance()
            load(b).wait()
            pending = [(b, piece) for piece in range(plan[b][1])]
    for item in pending:
        multiply(*item)
    for _ in stages:
        advance()
    attend()
    for dz in range(1, deep):
        @pl.when(z + dz < deep)
        def _():
            z_sum_copy(dz).wait_send()
    for copy in sent:
        copy.wait_send()


def gather_multiply(x, w, deep, wide, room):
    tokens, channels = x.shape
    depth, columns = w.shape
    plan = round_plan(columns // LANES)
    rounds = len(plan)
    dma = pltpu.SemaphoreType.DMA
    half, f32 = HEADS // 2, jnp.float32
    attended, _ = pl.pallas_call(
        functools.partial(gather_kernel, plan, deep, wide, room),
        out_shape=(jax.ShapeDtypeStruct((tokens, HEADS * HEAD), jnp.bfloat16),
                   jax.ShapeDtypeStruct((channels, columns), jnp.bfloat16)),
        in_specs=[pl.BlockSpec(memory_space=pl.ANY), pl.BlockSpec(memory_space=pltpu.VMEM)],
        out_specs=(pl.BlockSpec(memory_space=pltpu.VMEM), pl.BlockSpec(memory_space=pl.ANY)),
        scratch_shapes=[
            pltpu.VMEM((tokens, channels), jnp.bfloat16),
            pltpu.VMEM((2, channels, 2 * CLASSES * LANES), jnp.bfloat16),
            pltpu.VMEM((tokens, columns), jnp.bfloat16),
            pltpu.VMEM((HEADS, HEAD, LANES), f32),
            pltpu.VMEM((half, HEAD, LANES), f32),
            pltpu.VMEM((half, HEAD, LANES), f32),
            pltpu.VMEM((half, HEAD // 2, LANES), f32),
            pltpu.VMEM((half, HEAD // 2, LANES), f32),
            pltpu.VMEM((deep, half, HEAD // 2, LANES), f32),
            pltpu.VMEM((half, HEAD // 2, LANES), f32),
            pltpu.VMEM((HEADS, HEAD, LANES), f32),
            pltpu.VMEM((HEADS, LANES, LANES), jnp.bfloat16),
            dma, dma((rounds, CLASSES)), dma((2,)),
            dma((rounds, 2, deep)), dma((rounds, 2, deep)),
            dma((rounds, 2, deep)), dma((rounds, 2, deep)),
            dma((rounds, 2, deep)), dma((rounds, 2, deep)),
            dma((rounds, 3)), dma((rounds, 3)),
            dma((deep + 3,)), dma((deep + 3,)),
        ],
        compiler_params=pltpu.CompilerParams(
            collective_id=0, has_side_effects=True, vmem_limit_bytes=56 * 2 ** 20),
        name="gather_multiply",
    )(x, w)
    return attended


def own_share(states, key_sums):
    both = jnp.concatenate([states, key_sums[:, :, None]], axis=2)
    both = lax.psum(both, "space")
    pieces = lax.all_gather(both, "tm")
    place = lax.broadcasted_iota(jnp.int32, (pieces.shape[0], 1, 1, 1), 0)
    total = jnp.sum(jnp.where(place <= lax.axis_index("tm"), pieces, 0.0), axis=0)
    return total[:, :, :HEAD], total[:, :, HEAD]


def on_device(deep, wide, latents, proj_weight):
    frame_count, band_rows, column_count, channels = latents.shape
    flat = latents.reshape(-1, channels)
    depth, columns = proj_weight.shape
    part = HEADS * HEAD
    queries, keys, values = (proj_weight[:, i * part:(i + 1) * part] for i in range(3))
    if wide:
        room = -(-part // LANES) * LANES
        total = 2 * CLASSES * LANES * ((3 * room) // (2 * CLASSES * LANES))
        total += -(-(3 * room - total) // (4 * LANES)) * 4 * LANES
        gap = ((0, 0), (0, room - part))
        packed = jnp.concatenate(
            [jnp.pad(keys, gap), jnp.pad(values, gap), jnp.pad(queries, ((0, 0), (0, total - 2 * room - part)))], axis=1)
        attended = gather_multiply(flat, packed, deep, wide, room)
        return attended.reshape(frame_count, band_rows, column_count, part)
    full = lax.all_gather(proj_weight, "tm", axis=0, tiled=True)
    projected = jnp.dot(flat, full, preferred_element_type=jnp.float32).astype(jnp.bfloat16)
    queries, keys, values = (projected[:, i * part:(i + 1) * part] for i in range(3))
    queries, keys, values = (a.reshape(-1, HEADS, HEAD) for a in (queries, keys, values))
    queries, keys = jax.nn.relu(queries), jax.nn.relu(keys)
    states = jnp.einsum("nhe,nhf->hef", keys, values, preferred_element_type=jnp.float32)
    key_sums = jnp.sum(keys, axis=0, dtype=jnp.float32)
    states, key_sums = own_share(states, key_sums)
    numerator = jnp.einsum(
        "nhe,hef->nhf", queries, states.astype(jnp.bfloat16), preferred_element_type=jnp.float32)
    denominator = jnp.einsum(
        "nhe,he->nh", queries.astype(jnp.float32), key_sums, precision=lax.Precision.HIGHEST)
    attended = (numerator / (denominator[:, :, None] + 1.0)).astype(jnp.bfloat16)
    return attended.reshape(frame_count, band_rows, column_count, part)


def solution(mesh):
    groups, blocks, bands = (mesh.shape[a] for a in ("groups", "tm", "space"))
    wide = 2

    def body(latents, proj_weight):
        fits = (groups == 2 and bands == 2 and blocks % wide == 0 and proj_weight.shape[0] % 8 == 0)
        return on_device(blocks // wide, wide if fits else 0, latents, proj_weight)

    return jax.shard_map(
        body,
        mesh=mesh,
        in_specs=(P(("groups", "tm"), "space", None, None), P("tm", None)),
        out_specs=P(("groups", "tm"), "space", None, None),
        check_vma=False,
    )
```

```python
import functools

import jax
import jax.numpy as jnp
from jax import lax
from jax.experimental import pallas as pl
from jax.experimental.pallas import tpu as pltpu
from jax.sharding import PartitionSpec as P

HEADS = 10
HEAD = 112
LANES = 128
MESH = pl.DeviceIdType.MESH


def unit_plan(units, early):
    split = units // 3
    split_early = early * 3 // 10
    both_early = early - 2 * split_early
    pairs = [2 * m if m < split_early else early + 2 * (m - split_early) for m in range(split)]
    both = [2 * split_early + m for m in range(both_early)]
    both += list(range(early + 2 * (split - split_early), units))
    order = [("mine", m) for m in range(split_early)] + [("both", m) for m in range(both_early)]
    order += [("mine", m) for m in range(split_early, split)] + [("both", m) for m in range(both_early, len(both))]
    return pairs, both, order


def gather_kernel(plan, early, deep, wide, x_hbm, w_ref, o_ref, buf, x_vm, w_vm, q_ref,
                  local, from_core, block_sum, from_y, pair_sum, from_z, to_y, totals, rounded,
                  x_sem, own_sem, load_sem, zs, zr, ys, yr, xs, xr, cs, cr, ss, sr):
    group, t, core = lax.axis_index("groups"), lax.axis_index("tm"), lax.axis_index("space")
    z, y = t // wide, t % wide
    own_class = group % 2
    depth = w_ref.shape[0]
    x_peer = {"groups": group + 1 - 2 * own_class}
    y_peer = {"tm": z * wide + 1 - y}
    core_peer = {"space": 1 - core}

    def z_at(dz):
        return lax.rem(z + deep - dz, deep)

    barrier = pltpu.get_barrier_semaphore()
    peers = [x_peer, y_peer, core_peer]
    peers += [{"tm": lax.rem(z + dz, deep) * wide + y} for dz in range(1, deep)]
    for peer in peers:
        pl.semaphore_signal(barrier, inc=1, device_id=peer, device_id_type=MESH)

    x_copy = pltpu.make_async_copy(x_hbm, x_vm, x_sem)
    x_copy.start()

    pairs, both, order = plan
    units = 2 * len(pairs) + len(both)
    step = 2 * LANES
    depth_of_split = len(pairs)

    def unit(kind, m):
        if kind == "both":
            return both[m]
        return pairs[m] + (own_class if kind == "mine" else 1 - own_class)

    def slot(kind, m):
        return {"mine": 0, "both": depth_of_split, "other": depth_of_split + len(both)}[kind] + m

    def cols(kind, m):
        return pl.ds(pl.multiple_of(unit(kind, m) * step + core * LANES, LANES), LANES)

    def rows(shard):
        return pl.ds(pl.multiple_of(shard * depth, 8), depth)

    everything = order + [("other", m) for m in range(depth_of_split)]

    def own_copy(kind, m):
        c = cols(kind, m)
        return pltpu.make_async_copy(w_ref.at[:, c], buf.at[rows(t), c], own_sem.at[slot(kind, m)])

    for tile in everything:
        own_copy(*tile).start()

    pl.semaphore_wait(barrier, len(peers))

    def remote(src, dst, send, recv, peer):
        return pltpu.make_async_remote_copy(
            src_ref=src, dst_ref=dst, send_sem=send, recv_sem=recv,
            device_id=peer, device_id_type=MESH)

    def z_copy(kind, m, dz):
        c, n = cols(kind, m), slot(kind, m)
        return remote(w_ref.at[:, c], buf.at[rows(t), c], zs.at[n, dz], zr.at[n, dz],
                      {"tm": lax.rem(z + dz, deep) * wide + y})

    def y_copy(kind, m, dz):
        c, n = cols(kind, m), slot(kind, m)
        at = buf.at[rows(z_at(dz) * wide + y), c]
        return remote(w_ref.at[:, c] if dz == 0 else at, at, ys.at[n, dz], yr.at[n, dz], y_peer)

    def x_pass(m, dz, side):
        at = buf.at[rows(z_at(dz) * wide + (y if side == 0 else 1 - y)), cols("mine", m)]
        return remote(at, at, xs.at[m, side, dz], xr.at[m, side, dz], x_peer)

    def core_pass(kind, m):
        at, n = buf.at[:, cols(kind, m)], slot(kind, m)
        return remote(at, at, cs.at[n], cr.at[n], core_peer)

    sent = []

    def start(copy):
        copy.start()
        sent.append(copy)

    def load(kind, m):
        n = slot(kind, m)
        c = pl.ds(pl.multiple_of(unit(kind, m) * step, step), step)
        return pltpu.make_async_copy(buf.at[:, c], w_vm.at[n], load_sem.at[n])

    block = 240

    tokens = x_vm.shape[0]
    half = HEADS // 2
    rows_half = HEAD // 2
    my_heads, other_heads = pl.ds(core * half, half), pl.ds((1 - core) * half, half)
    my_rows = pl.ds(pl.multiple_of(y * rows_half, 8), rows_half)
    other_rows = pl.ds(pl.multiple_of((1 - y) * rows_half, 8), rows_half)

    lane_of = lax.broadcasted_iota(jnp.int32, (block, LANES), 1)

    def multiply(kind, m):
        n, u = slot(kind, m), unit(kind, m)

        def project(i):
            at = pl.ds(pl.multiple_of(i * block, block), block)
            return at, jnp.dot(x_vm[at, :], w_vm[n], preferred_element_type=jnp.float32).astype(jnp.bfloat16)

        def keys_values(i, total):
            _, both_parts = project(i)
            keys = jnp.maximum(both_parts[:, :LANES], 0)
            values = both_parts[:, LANES:]
            values = jnp.where(lane_of < HEAD, values, jnp.ones_like(values))
            return total + lax.dot_general(
                keys, values, (((0,), (0,)), ((), ())), preferred_element_type=jnp.float32)

        def queries(i, carry):
            at, part = project(i)
            q_ref[u - early, at, :] = jnp.maximum(part, 0)
            return carry

        is_early = m < (sum(p < early for p in pairs) if kind != "both" else sum(p < early for p in both))
        if is_early:
            total = lax.fori_loop(0, tokens // block, keys_values, jnp.zeros((LANES, LANES), jnp.float32))
            local[u] = total[:HEAD]
        else:
            lax.fori_loop(0, tokens // block, queries, 0)

    def block_states_and_send():
        start(core_sum_copy())

    def core_sum_copy():
        return remote(local.at[other_heads], from_core, ss.at[0], sr.at[0], core_peer)

    def y_sum_copy():
        return remote(block_sum.at[:, other_rows], from_y, ss.at[1], sr.at[1], y_peer)

    def z_sum_copy(dz):
        return remote(pair_sum, from_z.at[dz], ss.at[3 + dz], sr.at[3 + dz],
                      {"tm": lax.rem(z + dz, deep) * wide + y})

    def y_total_copy():
        return remote(to_y, totals.at[my_heads, my_rows], ss.at[2], sr.at[2], y_peer)

    def core_total_copy():
        return remote(totals.at[my_heads], totals.at[my_heads], ss.at[3], sr.at[3], core_peer)

    def exchange_core():
        core_sum_copy().wait_recv()
        block_sum[...] = local[my_heads] + from_core[...]
        start(y_sum_copy())

    def exchange_y():
        y_sum_copy().wait_recv()
        pair_sum[...] = block_sum[:, my_rows] + from_y[...]
        for dz in range(1, deep):
            @pl.when(z + dz < deep)
            def _():
                z_sum_copy(dz).start()

    def exchange_z():
        earlier_me = block_sum[:, my_rows] + jnp.where(y == 0, 0.0, from_y[...])
        earlier_peer = from_y[...] + jnp.where(y == 0, block_sum[:, my_rows], 0.0)
        totals[my_heads, my_rows] = earlier_me
        to_y[...] = earlier_peer
        for dz in range(1, deep):
            @pl.when(z >= dz)
            def _():
                z_sum_copy(dz).wait_recv()
                totals[my_heads, my_rows] += from_z[dz]
                to_y[...] += from_z[dz]
        start(y_total_copy())

    def exchange_back():
        y_total_copy().wait_recv()
        start(core_total_copy())

    def attend():
        core_total_copy().wait_recv()
        lane = lax.broadcasted_iota(jnp.int32, (HEAD, LANES), 1)
        for h in range(HEADS):
            total = totals[h]
            sums = jnp.broadcast_to(total[:, HEAD:HEAD + 1], (HEAD, LANES))
            high = sums.astype(jnp.bfloat16).astype(jnp.float32)
            middle = (sums - high).astype(jnp.bfloat16).astype(jnp.float32)
            low = sums - high - middle
            tail = jnp.where(lane == HEAD, high, jnp.where(lane == HEAD + 1, middle, jnp.where(lane == HEAD + 2, low, 0.0)))
            rounded[h, :HEAD] = jnp.where(lane < HEAD, total, tail).astype(jnp.bfloat16)

        def body(i, carry):
            at = pl.ds(pl.multiple_of(i * block, block), block)
            for h in range(HEADS):
                first, last = h * HEAD, h * HEAD + HEAD
                head = first // step
                if last <= (head + 1) * step:
                    queries = q_ref[head, at, first - head * step:last - head * step]
                else:
                    queries = jnp.concatenate(
                        [q_ref[head, at, first - head * step:], q_ref[head + 1, at, :last - (head + 1) * step]], axis=1)
                out = jnp.dot(queries, rounded[h, :HEAD], preferred_element_type=jnp.float32)
                below = out[:, HEAD:HEAD + 1] + out[:, HEAD + 1:HEAD + 2] + out[:, HEAD + 2:HEAD + 3] + 1.0
                o_ref[at, h * HEAD:(h + 1) * HEAD] = (out[:, :HEAD] / below).astype(o_ref.dtype)
            return carry

        lax.fori_loop(0, tokens // block, body, 0)

    events = []

    def event(when, action):
        events.append((when, len(events), action))

    tile_time, hop = 6.3, 2.5

    def send_own(tile):
        for dz in range(1, deep):
            start(z_copy(*tile, dz))
        start(y_copy(*tile, 0))

    def from_z_tile(tile, dz):
        z_copy(*tile, dz).wait_recv()
        start(y_copy(*tile, dz))
        if tile[0] == "mine":
            start(x_pass(tile[1], dz, 0))

    def from_y_tile(tile, dz):
        y_copy(*tile, dz).wait_recv()
        if tile[0] == "mine":
            start(x_pass(tile[1], dz, 1))

    def from_x_tile(m, dz, side):
        x_pass(m, dz, side).wait_recv()

    def to_core(tile):
        own_copy(*tile).wait()
        start(core_pass(*tile))

    def from_core_tile(tile):
        core_pass(*tile).wait_recv()
        load(*tile).start()

    def run(tile):
        load(*tile).wait()
        multiply(*tile)

    def finish(tile, when):
        event(when, functools.partial(to_core, tile))
        event(when + hop, functools.partial(from_core_tile, tile))
        event(when + 2 * hop, functools.partial(run, tile))
        is_kv = tile[1] < (sum(p < early for p in (both if tile[0] == "both" else pairs)))
        return when + 2 * hop if is_kv else 0.0

    ready, x_end = 0.0, 0.0
    for i, tile in enumerate(order):
        base = i * tile_time
        event(max(base - 2 * tile_time, -1.0), functools.partial(send_own, tile))
        for dz in range(1, deep):
            event(base + dz * tile_time / (deep - 1), functools.partial(from_z_tile, tile, dz))
        for dz in range(deep):
            event(base + dz * tile_time / (deep - 1) + hop, functools.partial(from_y_tile, tile, dz))
        complete = base + tile_time + hop
        ready = max(ready, finish(tile, complete + 0.1))
        if tile[0] == "mine":
            x_end = max(x_end + 11.5, complete + 4.0)
            for dz in range(1, deep):
                event(x_end - 0.1, functools.partial(from_x_tile, tile[1], dz, 0))
            for dz in range(deep):
                event(x_end - 0.1, functools.partial(from_x_tile, tile[1], dz, 1))
            ready = max(ready, finish(("other", tile[1]), x_end))
    for stage, delay in ((block_states_and_send, 0.1), (exchange_core, 2.0), (exchange_y, 6.0),
                         (exchange_z, 18.0), (exchange_back, 22.0)):
        event(ready + delay, stage)
    events.sort(key=lambda e: e[:2])
    x_copy.wait()
    for _, _, action in events:
        action()
    attend()
    for dz in range(1, deep):
        @pl.when(z + dz < deep)
        def _():
            z_sum_copy(dz).wait_send()
    for copy in sent:
        copy.wait_send()


def gather_multiply(x, w, deep, wide, early):
    tokens, channels = x.shape
    depth, columns = w.shape
    step = 2 * LANES
    units = columns // step
    plan = unit_plan(units, early)
    split, fetched = len(plan[0]), len(plan[2])
    dma = pltpu.SemaphoreType.DMA
    half, f32 = HEADS // 2, jnp.float32
    attended, _ = pl.pallas_call(
        functools.partial(gather_kernel, plan, early, deep, wide),
        out_shape=(jax.ShapeDtypeStruct((tokens, HEADS * HEAD), jnp.bfloat16),
                   jax.ShapeDtypeStruct((channels, columns), jnp.bfloat16)),
        in_specs=[pl.BlockSpec(memory_space=pl.ANY), pl.BlockSpec(memory_space=pltpu.VMEM)],
        out_specs=(pl.BlockSpec(memory_space=pltpu.VMEM), pl.BlockSpec(memory_space=pl.ANY)),
        scratch_shapes=[
            pltpu.VMEM((tokens, channels), jnp.bfloat16),
            pltpu.VMEM((units, channels, step), jnp.bfloat16),
            pltpu.VMEM((units - early, tokens, step), jnp.bfloat16),
            pltpu.VMEM((HEADS, HEAD, LANES), f32),
            pltpu.VMEM((half, HEAD, LANES), f32),
            pltpu.VMEM((half, HEAD, LANES), f32),
            pltpu.VMEM((half, HEAD // 2, LANES), f32),
            pltpu.VMEM((half, HEAD // 2, LANES), f32),
            pltpu.VMEM((deep, half, HEAD // 2, LANES), f32),
            pltpu.VMEM((half, HEAD // 2, LANES), f32),
            pltpu.VMEM((HEADS, HEAD, LANES), f32),
            pltpu.VMEM((HEADS, HEAD, LANES), jnp.bfloat16),
            dma, dma((units,)), dma((units,)),
            dma((fetched, deep)), dma((fetched, deep)),
            dma((fetched, deep)), dma((fetched, deep)),
            dma((split, 2, deep)), dma((split, 2, deep)),
            dma((units,)), dma((units,)),
            dma((deep + 3,)), dma((deep + 3,)),
        ],
        compiler_params=pltpu.CompilerParams(
            collective_id=0, has_side_effects=True, vmem_limit_bytes=56 * 2 ** 20),
        name="gather_multiply",
    )(x, w)
    return attended


def own_share(states, key_sums):
    both = jnp.concatenate([states, key_sums[:, :, None]], axis=2)
    both = lax.psum(both, "space")
    pieces = lax.all_gather(both, "tm")
    place = lax.broadcasted_iota(jnp.int32, (pieces.shape[0], 1, 1, 1), 0)
    total = jnp.sum(jnp.where(place <= lax.axis_index("tm"), pieces, 0.0), axis=0)
    return total[:, :, :HEAD], total[:, :, HEAD]


def on_device(deep, wide, latents, proj_weight):
    frame_count, band_rows, column_count, channels = latents.shape
    flat = latents.reshape(-1, channels)
    depth, columns = proj_weight.shape
    part = HEADS * HEAD
    queries, keys, values = (proj_weight[:, i * part:(i + 1) * part] for i in range(3))
    if wide:
        gap = ((0, 0), (0, 0), (0, LANES - HEAD))
        pads = [jnp.pad(a.reshape(depth, HEADS, HEAD), gap) for a in (keys, values)]
        heads = jnp.stack(pads, axis=2).reshape(depth, 2 * HEADS * LANES)
        step = 2 * LANES
        rest = -(-part // step) * step
        packed = jnp.concatenate([heads, jnp.pad(queries, ((0, 0), (0, rest - part)))], axis=1)
        attended = gather_multiply(flat, packed, deep, wide, HEADS)
        return attended.reshape(frame_count, band_rows, column_count, part)
    full = lax.all_gather(proj_weight, "tm", axis=0, tiled=True)
    projected = jnp.dot(flat, full, preferred_element_type=jnp.float32).astype(jnp.bfloat16)
    queries, keys, values = (projected[:, i * part:(i + 1) * part] for i in range(3))
    queries, keys, values = (a.reshape(-1, HEADS, HEAD) for a in (queries, keys, values))
    queries, keys = jax.nn.relu(queries), jax.nn.relu(keys)
    states = jnp.einsum("nhe,nhf->hef", keys, values, preferred_element_type=jnp.float32)
    key_sums = jnp.sum(keys, axis=0, dtype=jnp.float32)
    states, key_sums = own_share(states, key_sums)
    numerator = jnp.einsum(
        "nhe,hef->nhf", queries, states.astype(jnp.bfloat16), preferred_element_type=jnp.float32)
    denominator = jnp.einsum(
        "nhe,he->nh", queries.astype(jnp.float32), key_sums, precision=lax.Precision.HIGHEST)
    attended = (numerator / (denominator[:, :, None] + 1.0)).astype(jnp.bfloat16)
    return attended.reshape(frame_count, band_rows, column_count, part)


def solution(mesh):
    groups, blocks, bands = (mesh.shape[a] for a in ("groups", "tm", "space"))
    wide = 2

    def body(latents, proj_weight):
        fits = (groups == 2 and bands == 2 and blocks % wide == 0 and proj_weight.shape[0] % 8 == 0)
        return on_device(blocks // wide, wide if fits else 0, latents, proj_weight)

    return jax.shard_map(
        body,
        mesh=mesh,
        in_specs=(P(("groups", "tm"), "space", None, None), P("tm", None)),
        out_specs=P(("groups", "tm"), "space", None, None),
        check_vma=False,
    )
```

```python
import functools

import jax
import jax.numpy as jnp
from jax import lax
from jax.experimental import pallas as pl
from jax.experimental.pallas import tpu as pltpu
from jax.sharding import PartitionSpec as P

HEADS = 10
HEAD = 112
LANES = 128
MESH = pl.DeviceIdType.MESH


def unit_plan(units, early):
    split = units // 3
    split_early = early * 3 // 10
    both_early = early - 2 * split_early
    pairs = [2 * m if m < split_early else early + 2 * (m - split_early) for m in range(split)]
    both = [2 * split_early + m for m in range(both_early)]
    both += list(range(early + 2 * (split - split_early), units))
    order = [("mine", m) for m in range(split_early)] + [("both", m) for m in range(both_early)]
    order += [("mine", m) for m in range(split_early, split)] + [("both", m) for m in range(both_early, len(both))]
    return pairs, both, order


def gather_kernel(plan, early, deep, wide, x_hbm, raw_ref, o_ref, buf, x_vm, w_vm, q_ref, w_ref,
                  local, from_core, block_sum, from_y, pair_sum, from_z, to_y, totals, rounded,
                  x_sem, own_sem, load_sem, zs, zr, ys, yr, xs, xr, cs, cr, ss, sr):
    group, t, core = lax.axis_index("groups"), lax.axis_index("tm"), lax.axis_index("space")
    z, y = t // wide, t % wide
    own_class = group % 2
    depth = w_ref.shape[0]
    x_peer = {"groups": group + 1 - 2 * own_class}
    y_peer = {"tm": z * wide + 1 - y}
    core_peer = {"space": 1 - core}

    def z_at(dz):
        return lax.rem(z + deep - dz, deep)

    barrier = pltpu.get_barrier_semaphore()
    peers = [x_peer, y_peer, core_peer]
    peers += [{"tm": lax.rem(z + dz, deep) * wide + y} for dz in range(1, deep)]
    for peer in peers:
        pl.semaphore_signal(barrier, inc=1, device_id=peer, device_id_type=MESH)

    x_copy = pltpu.make_async_copy(x_hbm, x_vm, x_sem)
    x_copy.start()

    pairs, both, order = plan
    units = 2 * len(pairs) + len(both)
    step = 2 * LANES
    depth_of_split = len(pairs)

    def unit(kind, m):
        if kind == "both":
            return both[m]
        return pairs[m] + (own_class if kind == "mine" else 1 - own_class)

    def slot(kind, m):
        return {"mine": 0, "both": depth_of_split, "other": depth_of_split + len(both)}[kind] + m

    def cols(kind, m):
        return pl.ds(pl.multiple_of(unit(kind, m) * step + core * LANES, LANES), LANES)

    def rows(shard):
        return pl.ds(pl.multiple_of(shard * depth, 8), depth)

    everything = order + [("other", m) for m in range(depth_of_split)]

    def own_copy(kind, m):
        c = cols(kind, m)
        return pltpu.make_async_copy(w_ref.at[:, c], buf.at[rows(t), c], own_sem.at[slot(kind, m)])

    part = HEADS * HEAD
    for i in range(2):
        for h in range(HEADS):
            first = (i + 1) * part + h * HEAD
            piece = raw_ref[:, first:min(first + LANES, 3 * part)]
            if piece.shape[1] < LANES:
                piece = jnp.concatenate([piece, jnp.zeros((depth, LANES - piece.shape[1]), piece.dtype)], axis=1)
            w_ref[:, h * step + i * LANES:h * step + (i + 1) * LANES] = piece
    aligned = part // LANES * LANES
    w_ref[:, early * step:early * step + aligned] = raw_ref[:, :aligned]
    w_ref[:, early * step + aligned:] = jnp.concatenate(
        [raw_ref[:, aligned:part], jnp.zeros((depth, w_ref.shape[1] - early * step - part), w_ref.dtype)], axis=1)
    for tile in everything:
        own_copy(*tile).start()

    pl.semaphore_wait(barrier, len(peers))

    def remote(src, dst, send, recv, peer):
        return pltpu.make_async_remote_copy(
            src_ref=src, dst_ref=dst, send_sem=send, recv_sem=recv,
            device_id=peer, device_id_type=MESH)

    def z_copy(kind, m, dz):
        c, n = cols(kind, m), slot(kind, m)
        return remote(w_ref.at[:, c], buf.at[rows(t), c], zs.at[n, dz], zr.at[n, dz],
                      {"tm": lax.rem(z + dz, deep) * wide + y})

    def y_copy(kind, m, dz):
        c, n = cols(kind, m), slot(kind, m)
        at = buf.at[rows(z_at(dz) * wide + y), c]
        return remote(w_ref.at[:, c] if dz == 0 else at, at, ys.at[n, dz], yr.at[n, dz], y_peer)

    def x_pass(m, dz, side):
        at = buf.at[rows(z_at(dz) * wide + (y if side == 0 else 1 - y)), cols("mine", m)]
        return remote(at, at, xs.at[m, side, dz], xr.at[m, side, dz], x_peer)

    def core_pass(kind, m):
        at, n = buf.at[:, cols(kind, m)], slot(kind, m)
        return remote(at, at, cs.at[n], cr.at[n], core_peer)

    sent = []

    def start(copy):
        copy.start()
        sent.append(copy)

    def load(kind, m):
        n = slot(kind, m)
        c = pl.ds(pl.multiple_of(unit(kind, m) * step, step), step)
        return pltpu.make_async_copy(buf.at[:, c], w_vm.at[n], load_sem.at[n])

    block = 240

    tokens = x_vm.shape[0]
    half = HEADS // 2
    rows_half = HEAD // 2
    my_heads, other_heads = pl.ds(core * half, half), pl.ds((1 - core) * half, half)
    my_rows = pl.ds(pl.multiple_of(y * rows_half, 8), rows_half)
    other_rows = pl.ds(pl.multiple_of((1 - y) * rows_half, 8), rows_half)

    lane_of = lax.broadcasted_iota(jnp.int32, (block, LANES), 1)

    def multiply(kind, m):
        n, u = slot(kind, m), unit(kind, m)

        def project(i):
            at = pl.ds(pl.multiple_of(i * block, block), block)
            return at, jnp.dot(x_vm[at, :], w_vm[n], preferred_element_type=jnp.float32).astype(jnp.bfloat16)

        def keys_values(i, total):
            _, both_parts = project(i)
            keys = jnp.maximum(both_parts[:, :LANES], 0)
            values = both_parts[:, LANES:]
            values = jnp.where(lane_of < HEAD, values, jnp.ones_like(values))
            return total + lax.dot_general(
                keys, values, (((0,), (0,)), ((), ())), preferred_element_type=jnp.float32)

        def queries(i, carry):
            at, part = project(i)
            q_ref[u - early, at, :] = jnp.maximum(part, 0)
            return carry

        is_early = m < (sum(p < early for p in pairs) if kind != "both" else sum(p < early for p in both))
        if is_early:
            total = lax.fori_loop(0, tokens // block, keys_values, jnp.zeros((LANES, LANES), jnp.float32))
            local[u] = total[:HEAD]
        else:
            lax.fori_loop(0, tokens // block, queries, 0)

    def block_states_and_send():
        start(core_sum_copy())

    def core_sum_copy():
        return remote(local.at[other_heads], from_core, ss.at[0], sr.at[0], core_peer)

    def y_sum_copy():
        return remote(block_sum.at[:, other_rows], from_y, ss.at[1], sr.at[1], y_peer)

    def z_sum_copy(dz):
        return remote(pair_sum, from_z.at[dz], ss.at[3 + dz], sr.at[3 + dz],
                      {"tm": lax.rem(z + dz, deep) * wide + y})

    def y_total_copy():
        return remote(to_y, totals.at[my_heads, my_rows], ss.at[2], sr.at[2], y_peer)

    def core_total_copy():
        return remote(totals.at[my_heads], totals.at[my_heads], ss.at[3], sr.at[3], core_peer)

    def exchange_core():
        core_sum_copy().wait_recv()
        block_sum[...] = local[my_heads] + from_core[...]
        start(y_sum_copy())

    def exchange_y():
        y_sum_copy().wait_recv()
        pair_sum[...] = block_sum[:, my_rows] + from_y[...]
        for dz in range(1, deep):
            @pl.when(z + dz < deep)
            def _():
                z_sum_copy(dz).start()

    def exchange_z():
        earlier_me = block_sum[:, my_rows] + jnp.where(y == 0, 0.0, from_y[...])
        earlier_peer = from_y[...] + jnp.where(y == 0, block_sum[:, my_rows], 0.0)
        totals[my_heads, my_rows] = earlier_me
        to_y[...] = earlier_peer
        for dz in range(1, deep):
            @pl.when(z >= dz)
            def _():
                z_sum_copy(dz).wait_recv()
                totals[my_heads, my_rows] += from_z[dz]
                to_y[...] += from_z[dz]
        start(y_total_copy())

    def exchange_back():
        y_total_copy().wait_recv()
        start(core_total_copy())

    def attend():
        core_total_copy().wait_recv()
        lane = lax.broadcasted_iota(jnp.int32, (HEAD, LANES), 1)
        for h in range(HEADS):
            total = totals[h]
            sums = jnp.broadcast_to(total[:, HEAD:HEAD + 1], (HEAD, LANES))
            high = sums.astype(jnp.bfloat16).astype(jnp.float32)
            middle = (sums - high).astype(jnp.bfloat16).astype(jnp.float32)
            low = sums - high - middle
            tail = jnp.where(lane == HEAD, high, jnp.where(lane == HEAD + 1, middle, jnp.where(lane == HEAD + 2, low, 0.0)))
            rounded[h, :HEAD] = jnp.where(lane < HEAD, total, tail).astype(jnp.bfloat16)

        def body(i, carry):
            at = pl.ds(pl.multiple_of(i * block, block), block)
            for h in range(HEADS):
                first, last = h * HEAD, h * HEAD + HEAD
                head = first // step
                if last <= (head + 1) * step:
                    queries = q_ref[head, at, first - head * step:last - head * step]
                else:
                    queries = jnp.concatenate(
                        [q_ref[head, at, first - head * step:], q_ref[head + 1, at, :last - (head + 1) * step]], axis=1)
                out = jnp.dot(queries, rounded[h, :HEAD], preferred_element_type=jnp.float32)
                below = out[:, HEAD:HEAD + 1] + out[:, HEAD + 1:HEAD + 2] + out[:, HEAD + 2:HEAD + 3] + 1.0
                o_ref[at, h * HEAD:(h + 1) * HEAD] = (out[:, :HEAD] / below).astype(o_ref.dtype)
            return carry

        lax.fori_loop(0, tokens // block, body, 0)

    events = []

    def event(when, action):
        events.append((when, len(events), action))

    tile_time, hop = 8.0, 3.5

    def send_own(tile):
        for dz in range(1, deep):
            start(z_copy(*tile, dz))
        start(y_copy(*tile, 0))

    def from_z_tile(tile, dz):
        z_copy(*tile, dz).wait_recv()
        start(y_copy(*tile, dz))
        if tile[0] == "mine":
            start(x_pass(tile[1], dz, 0))

    def from_y_tile(tile, dz):
        y_copy(*tile, dz).wait_recv()
        if tile[0] == "mine":
            start(x_pass(tile[1], dz, 1))

    def from_x_tile(m, dz, side):
        x_pass(m, dz, side).wait_recv()

    def to_core(tile):
        own_copy(*tile).wait()
        start(core_pass(*tile))

    def from_core_tile(tile):
        core_pass(*tile).wait_recv()
        load(*tile).start()

    def run(tile):
        load(*tile).wait()
        multiply(*tile)

    def finish(tile, when):
        event(when, functools.partial(to_core, tile))
        event(when + hop, functools.partial(from_core_tile, tile))
        event(when + 2 * hop, functools.partial(run, tile))
        is_kv = tile[1] < (sum(p < early for p in (both if tile[0] == "both" else pairs)))
        return when + 2 * hop if is_kv else 0.0

    ready, x_end = 0.0, 0.0
    for i, tile in enumerate(order):
        base = i * tile_time
        event(max(base - 1 * tile_time, -1.0), functools.partial(send_own, tile))
        for dz in range(1, deep):
            event(base + dz * tile_time / (deep - 1), functools.partial(from_z_tile, tile, dz))
        for dz in range(deep):
            event(base + dz * tile_time / (deep - 1) + hop, functools.partial(from_y_tile, tile, dz))
        complete = base + tile_time + hop
        ready = max(ready, finish(tile, complete + 0.1))
        if tile[0] == "mine":
            x_end = max(x_end + 11.5, complete + 4.0)
            for dz in range(1, deep):
                event(x_end - 0.1, functools.partial(from_x_tile, tile[1], dz, 0))
            for dz in range(deep):
                event(x_end - 0.1, functools.partial(from_x_tile, tile[1], dz, 1))
            ready = max(ready, finish(("other", tile[1]), x_end))
    for stage, delay in ((block_states_and_send, 0.1), (exchange_core, 2.0), (exchange_y, 6.0),
                         (exchange_z, 18.0), (exchange_back, 22.0)):
        event(ready + delay, stage)
    events.sort(key=lambda e: e[:2])
    x_copy.wait()
    for _, _, action in events:
        action()
    attend()
    for dz in range(1, deep):
        @pl.when(z + dz < deep)
        def _():
            z_sum_copy(dz).wait_send()
    for copy in sent:
        copy.wait_send()


def gather_multiply(x, w, deep, wide, early):
    tokens, channels = x.shape
    depth = w.shape[0]
    step = 2 * LANES
    units = early - (-HEADS * HEAD // step)
    columns = units * step
    plan = unit_plan(units, early)
    split, fetched = len(plan[0]), len(plan[2])
    dma = pltpu.SemaphoreType.DMA
    half, f32 = HEADS // 2, jnp.float32
    attended, _ = pl.pallas_call(
        functools.partial(gather_kernel, plan, early, deep, wide),
        out_shape=(jax.ShapeDtypeStruct((tokens, HEADS * HEAD), jnp.bfloat16),
                   jax.ShapeDtypeStruct((channels, columns), jnp.bfloat16)),
        in_specs=[pl.BlockSpec(memory_space=pl.ANY), pl.BlockSpec(memory_space=pltpu.VMEM)],
        out_specs=(pl.BlockSpec(memory_space=pltpu.VMEM), pl.BlockSpec(memory_space=pl.ANY)),
        scratch_shapes=[
            pltpu.VMEM((tokens, channels), jnp.bfloat16),
            pltpu.VMEM((units, channels, step), jnp.bfloat16),
            pltpu.VMEM((units - early, tokens, step), jnp.bfloat16),
            pltpu.VMEM((depth, columns), jnp.bfloat16),
            pltpu.VMEM((HEADS, HEAD, LANES), f32),
            pltpu.VMEM((half, HEAD, LANES), f32),
            pltpu.VMEM((half, HEAD, LANES), f32),
            pltpu.VMEM((half, HEAD // 2, LANES), f32),
            pltpu.VMEM((half, HEAD // 2, LANES), f32),
            pltpu.VMEM((deep, half, HEAD // 2, LANES), f32),
            pltpu.VMEM((half, HEAD // 2, LANES), f32),
            pltpu.VMEM((HEADS, HEAD, LANES), f32),
            pltpu.VMEM((HEADS, HEAD, LANES), jnp.bfloat16),
            dma, dma((units,)), dma((units,)),
            dma((fetched, deep)), dma((fetched, deep)),
            dma((fetched, deep)), dma((fetched, deep)),
            dma((split, 2, deep)), dma((split, 2, deep)),
            dma((units,)), dma((units,)),
            dma((deep + 3,)), dma((deep + 3,)),
        ],
        compiler_params=pltpu.CompilerParams(
            collective_id=0, has_side_effects=True, vmem_limit_bytes=56 * 2 ** 20),
        name="gather_multiply",
    )(x, w)
    return attended


def own_share(states, key_sums):
    both = jnp.concatenate([states, key_sums[:, :, None]], axis=2)
    both = lax.psum(both, "space")
    pieces = lax.all_gather(both, "tm")
    place = lax.broadcasted_iota(jnp.int32, (pieces.shape[0], 1, 1, 1), 0)
    total = jnp.sum(jnp.where(place <= lax.axis_index("tm"), pieces, 0.0), axis=0)
    return total[:, :, :HEAD], total[:, :, HEAD]


def on_device(deep, wide, latents, proj_weight):
    frame_count, band_rows, column_count, channels = latents.shape
    flat = latents.reshape(-1, channels)
    part = HEADS * HEAD
    if wide:
        attended = gather_multiply(flat, proj_weight, deep, wide, HEADS)
        return attended.reshape(frame_count, band_rows, column_count, part)
    full = lax.all_gather(proj_weight, "tm", axis=0, tiled=True)
    projected = jnp.dot(flat, full, preferred_element_type=jnp.float32).astype(jnp.bfloat16)
    queries, keys, values = (projected[:, i * part:(i + 1) * part] for i in range(3))
    queries, keys, values = (a.reshape(-1, HEADS, HEAD) for a in (queries, keys, values))
    queries, keys = jax.nn.relu(queries), jax.nn.relu(keys)
    states = jnp.einsum("nhe,nhf->hef", keys, values, preferred_element_type=jnp.float32)
    key_sums = jnp.sum(keys, axis=0, dtype=jnp.float32)
    states, key_sums = own_share(states, key_sums)
    numerator = jnp.einsum(
        "nhe,hef->nhf", queries, states.astype(jnp.bfloat16), preferred_element_type=jnp.float32)
    denominator = jnp.einsum(
        "nhe,he->nh", queries.astype(jnp.float32), key_sums, precision=lax.Precision.HIGHEST)
    attended = (numerator / (denominator[:, :, None] + 1.0)).astype(jnp.bfloat16)
    return attended.reshape(frame_count, band_rows, column_count, part)


def solution(mesh):
    groups, blocks, bands = (mesh.shape[a] for a in ("groups", "tm", "space"))
    wide = 2

    def body(latents, proj_weight):
        fits = (groups == 2 and bands == 2 and blocks % wide == 0 and proj_weight.shape[0] % 8 == 0)
        return on_device(blocks // wide, wide if fits else 0, latents, proj_weight)

    return jax.shard_map(
        body,
        mesh=mesh,
        in_specs=(P(("groups", "tm"), "space", None, None), P("tm", None)),
        out_specs=P(("groups", "tm"), "space", None, None),
        check_vma=False,
    )
```
